512 devices in a mesh: sec: 32 (over x, z), mpo: 16 (over y, core).
Axes of the slice: x: 4, y: 8, z: 8, core: 2. Of those that a mesh axis runs over, the one named last changes fastest.
Arguments:
- psi_blocks: bfloat16 [256, 256, 256], P('sec'), may hold values from -6 to 6
- left_env: bfloat16 [64, 256, 256], P('mpo'), may hold values from -0.375 to 0.375
- right_env: bfloat16 [64, 256, 256], P('mpo'), may hold values from -0.046875 to 0.046875
- dest_index: int32 [16, 32, 32, 1], P('mpo', 'sec'), may hold values from 0 to 31; in each aligned block of 32 rows (0 to 31, 32 to 63, ..., all dimensions but the last counted through in order) at most 2 rows name the same one
- dest_slot: int32 [16, 32, 32], P('mpo', 'sec'), may hold values from 0 to 7
Outputs:
- sigma_blocks: float32 [256, 256, 256], P('sec', 'mpo')
The draws below stay inside these ranges and needn't reach their ends.
Inputs may be any that keep to these rules, and one draw needn't show every extreme that they name: `dest_index`: in the 32 pairs of one device (fixed j and i), at most 2 name the same index of sec, and some device has exactly 2 for one index.
All inputs are finite; a program needn't handle non-finite values.
Results may differ from the reference program's by a relative error of at most 0.0041.
Values may be sent and summed in bfloat16 or wider, within the bound.
No kernel may reach another device: no remote copies, remote signals or barrier semaphores. Data moves between devices by JAX's collectives and lax.ppermute only.
A program may use at most 128 MiB of HBM per device.

```python
import math
import jax
import jax.numpy as jnp
import numpy as np
from jax import lax

BD = 256
SEC_DEV = 8
TERM_DEV = 4
PAIRS = 32
CAP = 2
NSEC = 256
NTERM = 64
N_SEC = 32
N_MPO = 16


def with_ends(array, key, low, largest):
    index_at = [jax.random.randint(jax.random.fold_in(key, axis), (), 0, length) for axis, length in enumerate(array.shape)]
    longest = array.shape.index(max(array.shape))
    beside = index_at[:longest] + [(index_at[longest] + 1) % array.shape[longest]] + index_at[longest + 1:]
    return array.at[tuple(index_at)].set(low).at[tuple(beside)].set(largest)


def steps_of(stream_key, shape, shards, low, top_value):
    factor_of = 1.0
    for dim, parts in shards:
        heights = jax.random.uniform(jax.random.fold_in(jax.random.fold_in(stream_key, 6), dim), (parts,), jnp.float32, low / len(shards), top_value / len(shards))
        factor_of = factor_of * jnp.repeat(jnp.exp(heights), shape[dim] // parts).reshape((-1,) + (1,) * (len(shape) - 1 - dim))
    return factor_of


def routed_block(own_key, own, number, rows, number_of, top, reach, skew):
    ranking = jax.random.permutation(own_key, number_of)
    heavy_load, ordinary = portions_of(number_of, rows * top, reach, skew, True), portions_of(number_of, rows * top, reach, skew, False)
    places = jnp.arange(number_of)

    def named(sizes, turn):
        used = int((sizes > 0).sum())
        fixed = max(1, used // 4)
        shifted = fixed + (places - fixed + turn * (used - fixed)) % max(1, number_of - fixed)
        return jnp.zeros((number_of,), jnp.int32).at[ranking[jnp.where(places < fixed, places, shifted)]].set(jnp.asarray(sizes, jnp.int32))

    sizes = jnp.where(number % 4 == 0, named(heavy_load, number // 4), named(ordinary, number - number // 4 - 1))
    mixed = jax.random.permutation(jax.random.fold_in(own, 3), number_of)
    giver, receiver = mixed[0:number_of // 2 * 2:2], mixed[1:number_of // 2 * 2:2]
    slack = jnp.minimum(sizes[giver] - 1, reach - sizes[receiver]) // 2
    slack = jnp.where((giver == ranking[0]) | (receiver == ranking[0]) | (sizes[receiver] == 0), 0, jnp.maximum(slack, 0))
    shifted = jax.random.randint(jax.random.fold_in(own, 4), (number_of // 2,), 0, 1 << 20) % (slack + 1)
    sizes = sizes.at[giver].add(-shifted).at[receiver].add(shifted)
    members = jnp.searchsorted(jnp.cumsum(sizes), jnp.arange(rows * top), side="right").astype(jnp.int32)
    grid = members.reshape(top, rows).T
    grid = grid[jax.random.permutation(jax.random.fold_in(own, 1), rows)]
    turn = jax.random.randint(jax.random.fold_in(own, 2), (rows, 1), 0, top)
    return jnp.take_along_axis(grid, (jnp.arange(top)[None, :] + turn) % top, axis=1)


def portions_of(amount, total, most, skew, full):
    portions = [(1 << 20) // math.isqrt(standing ** skew) + 1 for standing in range(1, amount + 1)]
    largest = most if full else min(most, max(-(-total // amount), total * portions[0] // sum(portions)))
    least = 1 if total - largest >= amount - 1 else 0
    holding, spare = [largest] + [least] * (amount - 1), total - largest - least * (amount - 1)
    while spare > 0:
        movable = [i for i in range(1, amount) if holding[i] < largest] or [i for i in range(1, amount) if holding[i] < most]
        whole, budget = sum([portions[i] for i in movable]), spare
        for i in movable:
            addition = min(most - holding[i], max(1, budget * portions[i] // whole), spare)
            holding[i] = holding[i] + addition
            spare = spare - addition
    return np.array(holding)


def gaussian(stream_key, extent, spread, most, shards=(), held_as=jnp.bfloat16):
    result = jax.random.normal(stream_key, extent, jnp.float32) * spread
    if len(shards) > 0:
        result = steps_of(stream_key, extent, shards, -0.22, 0.18) * result
    return jnp.clip(result, min=-most, max=most).astype(held_as)


def setup_inputs(seed: int = 0) -> dict:
    keys = jax.random.split(jax.random.key(seed), 6)
    psi_blocks = gaussian(keys[0], (NSEC, BD, BD), 1.0, 6.0, ((0, 32),))
    left_env = gaussian(keys[1], (NTERM, BD, BD), BD ** -0.5, 0.375, ((0, 16),))
    right_env = gaussian(keys[2], (NTERM, BD, BD), (BD * NTERM) ** -0.5, 0.046875, ((0, 16),))
    dest_index_keys = jax.random.split(jax.random.fold_in(keys[3], 1), N_MPO * N_SEC * PAIRS // PAIRS)
    dest_index_turns = jax.random.permutation(jax.random.fold_in(keys[3], 3), N_MPO * N_SEC * PAIRS // PAIRS)
    dest_index = jax.vmap(lambda own, number: routed_block(jax.random.fold_in(keys[3], 2), own, number, PAIRS, N_SEC, 1, CAP, 2))(dest_index_keys, dest_index_turns).reshape((N_MPO, N_SEC, PAIRS, 1))
    dest_slot = with_ends(jax.random.randint(keys[4], (N_MPO, N_SEC, PAIRS), 0, SEC_DEV), jax.random.fold_in(keys[4], 1), 0, SEC_DEV - 1).astype(jnp.int32)
    return {"psi_blocks": psi_blocks, "left_env": left_env, "right_env": right_env, "dest_index": dest_index, "dest_slot": dest_slot}


def reference(psi_blocks, left_env, right_env, dest_index, dest_slot):
    width = psi_blocks.shape[1]
    total = jnp.zeros((NSEC, width, width), jnp.float32)

    def visit(carry, step):
        row = step // N_SEC
        col = step % N_SEC
        lefts = lax.dynamic_slice_in_dim(left_env, (row * TERM_DEV).astype(jnp.int32), TERM_DEV, 0).astype(jnp.float32)
        rights = lax.dynamic_slice_in_dim(right_env, (row * TERM_DEV).astype(jnp.int32), TERM_DEV, 0).astype(jnp.float32)
        sources = lax.dynamic_slice_in_dim(psi_blocks, (col * SEC_DEV).astype(jnp.int32), SEC_DEV, 0).astype(jnp.float32)
        half = jnp.einsum("wab,sbc->wsac", lefts, sources).astype(jnp.bfloat16)
        half = lax.optimization_barrier(half).astype(jnp.float32)
        full = jnp.einsum("wsac,wcd->wsad", half, rights).astype(jnp.bfloat16)
        target = dest_index[row, col, :, 0] * SEC_DEV + dest_slot[row, col]
        carry = carry.at[target.astype(jnp.int32)].add(full.reshape(PAIRS, width, width).astype(jnp.float32))
        return carry, None

    steps = jnp.arange(N_MPO * N_SEC, dtype=jnp.int32)
    total, unused = lax.scan(visit, total, steps)
    return total
```

```python
import jax
import jax.numpy as jnp
from jax import lax
from jax.sharding import PartitionSpec as P


def on_device(psi_blocks, left_env, right_env, dest_index, dest_slot):
    sectors = psi_blocks.shape[0]
    width = psi_blocks.shape[1]
    shards = lax.axis_size("sec")
    lefts = lax.all_to_all(left_env, "mpo", split_axis=1, concat_axis=0, tiled=True)
    rights = lax.all_gather(right_env, "mpo", axis=0, tiled=True)
    target = dest_index[:, :, :, 0] * sectors + dest_slot
    targets = lax.all_gather(target[0], "mpo", axis=0, tiled=True).reshape(-1)
    half = jnp.einsum("wrb,sbc->wsrc", lefts, psi_blocks, preferred_element_type=jnp.float32)
    half = half.astype(jnp.bfloat16)
    full = jnp.einsum("wsrc,wcd->wsrd", half, rights, preferred_element_type=jnp.float32)
    full = full.astype(jnp.bfloat16)
    rows = full.shape[2]
    select = jnp.arange(shards * sectors, dtype=jnp.int32)[:, None] == targets[None, :]
    partial = jnp.dot(
        select.astype(jnp.bfloat16),
        full.reshape(-1, rows * width),
        preferred_element_type=jnp.float32,
    )
    partial = partial.reshape(shards * sectors, rows, width)
    return lax.psum_scatter(partial, "sec", scatter_dimension=0, tiled=True)


def solution(mesh):
    in_specs = (
        P("sec", None, None),
        P("mpo", None, None),
        P("mpo", None, None),
        P("mpo", "sec", None, None),
        P("mpo", "sec", None),
    )
    out_specs = P("sec", "mpo", None)
    return jax.shard_map(
        on_device, mesh=mesh, in_specs=in_specs, out_specs=out_specs, check_vma=False
    )
```

```python
import jax
import jax.numpy as jnp
from jax import lax
from jax.sharding import PartitionSpec as P


def on_device(psi_blocks, left_env, right_env, dest_index, dest_slot):
    sectors = psi_blocks.shape[0]
    width = psi_blocks.shape[1]
    shards = lax.axis_size("sec")
    lefts = lax.all_to_all(left_env, "mpo", split_axis=1, concat_axis=0, tiled=True)
    rights = lax.all_gather(right_env, "mpo", axis=0, tiled=True)
    target = dest_index[:, :, :, 0] * sectors + dest_slot
    targets = lax.all_gather(target[0], "mpo", axis=0, tiled=True).reshape(-1)
    half = jnp.einsum("wrb,sbc->wsrc", lefts, psi_blocks, preferred_element_type=jnp.float32)
    half = half.astype(jnp.bfloat16)
    full = jnp.einsum("wsrc,wcd->wsrd", half, rights, preferred_element_type=jnp.float32)
    full = full.astype(jnp.bfloat16)
    rows = full.shape[2]
    select = jnp.arange(shards * sectors, dtype=jnp.int32)[:, None] == targets[None, :]
    partial = jnp.dot(
        select.astype(jnp.bfloat16),
        full.reshape(-1, rows * width),
        preferred_element_type=jnp.float32,
    )
    partial = partial.astype(jnp.bfloat16).reshape(shards * sectors, rows, width)
    received = lax.all_to_all(partial, "sec", split_axis=0, concat_axis=0, tiled=True)
    received = received.reshape(shards, sectors, rows, width)
    return jnp.sum(received.astype(jnp.float32), axis=0)


def solution(mesh):
    in_specs = (
        P("sec", None, None),
        P("mpo", None, None),
        P("mpo", None, None),
        P("mpo", "sec", None, None),
        P("mpo", "sec", None),
    )
    out_specs = P("sec", "mpo", None)
    return jax.shard_map(
        on_device, mesh=mesh, in_specs=in_specs, out_specs=out_specs, check_vma=False
    )
```

```python
import jax
import jax.numpy as jnp
from jax import lax
from jax.experimental import pallas as pl
from jax.experimental.pallas import tpu as pltpu
from jax.sharding import Mesh
from jax.sharding import PartitionSpec as P

X, Z, Y, C = 4, 8, 8, 2
SEC, MPO = ("x", "z"), ("y", "c")
BF16, F32 = jnp.bfloat16, jnp.float32
TAG_ROWS = 16
CAP = 2


def half_kernel(packet_ref, psi_ref, half_ref):
    shards, _, width = packet_ref.shape
    terms, _, rows, _ = half_ref.shape
    lefts = packet_ref[:, : terms // shards * rows, :].reshape(terms * rows, width)
    out = jnp.dot(lefts, psi_ref[0], preferred_element_type=F32).astype(BF16)
    half_ref[:, 0] = out.reshape(terms, rows, width)


def halves(packet, psi, terms, rows):
    count, width = psi.shape[:2]
    return pl.pallas_call(
        half_kernel,
        grid=(count,),
        in_specs=[
            pl.BlockSpec(packet.shape, lambda s: (0, 0, 0)),
            pl.BlockSpec((1, width, width), lambda s: (s, 0, 0)),
        ],
        out_specs=pl.BlockSpec((terms, 1, rows, width), lambda s: (0, s, 0, 0)),
        out_shape=jax.ShapeDtypeStruct((terms, count, rows, width), BF16),
        compiler_params=pltpu.CompilerParams(vmem_limit_bytes=32 << 20),
        cost_estimate=pl.CostEstimate(
            flops=2 * terms * rows * width * width * count,
            bytes_accessed=2 * count * width * (width + terms * rows),
            transcendentals=0,
        ),
        name="halves",
    )(packet, psi)


def sums_kernel(pair_ref, slot_ref, *refs):
    half_refs, (right_ref, out_ref, full_ref, total_ref) = refs[:-4], refs[-4:]
    step = pl.program_id(0)
    terms = right_ref.shape[0]
    rows, width = out_ref.shape[1:]
    sectors = full_ref.shape[0] // terms
    limit = pair_ref.shape[1]

    @pl.when(step == 0)
    def _():
        total_ref[...] = jnp.zeros_like(total_ref)

    for w in range(terms):
        at = w * sectors
        for half_ref in half_refs:
            count = half_ref.shape[1]
            lhs = half_ref[w].reshape(count * rows, width)
            full = jnp.dot(lhs, right_ref[w], preferred_element_type=F32).astype(BF16)
            full_ref[at : at + count] = full.astype(F32).reshape(count, rows, width)
            at += count
    for i in range(limit):
        total_ref[slot_ref[step, i]] += full_ref[pair_ref[step, i]]

    @pl.when(step == pl.num_programs(0) - 1)
    def _():
        out_ref[...] = total_ref[: out_ref.shape[0]].astype(BF16)


def sums(pairs, slots, halves_of, rights, shards, count):
    terms, _, rows, width = halves_of[0].shape
    each = terms // shards
    sectors = sum(h.shape[1] for h in halves_of)
    return pl.pallas_call(
        sums_kernel,
        grid_spec=pltpu.PrefetchScalarGridSpec(
            num_scalar_prefetch=2,
            grid=(shards,),
            in_specs=[
                pl.BlockSpec((each, h.shape[1], rows, width), lambda i, *_: (i, 0, 0, 0))
                for h in halves_of
            ]
            + [pl.BlockSpec((each, width, width), lambda i, *_: (i, 0, 0))],
            out_specs=pl.BlockSpec((count, rows, width), lambda i, *_: (0, 0, 0)),
            scratch_shapes=[
                pltpu.VMEM((each * sectors, rows, width), F32),
                pltpu.VMEM((count + 1, rows, width), F32),
            ],
        ),
        out_shape=jax.ShapeDtypeStruct((count, rows, width), BF16),
        compiler_params=pltpu.CompilerParams(vmem_limit_bytes=48 << 20),
        cost_estimate=pl.CostEstimate(
            flops=2 * terms * sectors * rows * width * width,
            bytes_accessed=2 * terms * width * (sectors * rows + width),
            transcendentals=0,
        ),
        name="sums",
    )(pairs, slots, *halves_of, rights)


def moved(block, axis, size, by):
    return lax.ppermute(block, axis, [(i, (i + by) % size) for i in range(size)])


def both_ways(block, axis, size, by):
    pairs = []
    for i in range(size):
        pairs.append((i * C, (i + by) % size * C))
        pairs.append((i * C + 1, (i - by) % size * C + 1))
    return lax.ppermute(block, (axis, "c"), pairs)


def added(parts):
    total = parts[0].astype(F32)
    for i in range(1, parts.shape[0]):
        total = total + parts[i].astype(F32)
    return total


def ending_here(targets, first, count, limit):
    number = targets.shape[1]
    here = (targets >= first) & (targets < first + count)
    before = jnp.arange(number)[:, None] < jnp.arange(number)[None, :]
    rank = jnp.dot(
        here.astype(BF16), before.astype(BF16), preferred_element_type=F32
    ).astype(jnp.int32)
    rank = jnp.where(here, rank, limit)
    chosen = rank[:, None, :] == jnp.arange(limit, dtype=jnp.int32)[None, :, None]
    pairs = jnp.sum(jnp.where(chosen, jnp.arange(number, dtype=jnp.int32), 0), axis=2)
    slots = jnp.sum(jnp.where(chosen, (targets - first - count)[:, None, :], 0), axis=2) + count
    return pairs, slots


def on_device(psi_blocks, left_env, right_env, dest_index, dest_slot):
    sectors, width = psi_blocks.shape[:2]
    terms = left_env.shape[0]
    shards = Y * C
    rows = width // shards
    part = sectors // C
    x, core = lax.axis_index("x"), lax.axis_index("c")
    rights = lax.all_gather(right_env, MPO, axis=0, tiled=True)
    psi_next = both_ways(psi_blocks, "x", X, 1)
    psi_far = both_ways(lax.dynamic_slice_in_dim(psi_blocks, core * part, part, 0), "x", X, 2)
    psi_a = jnp.concatenate([psi_next, psi_far])
    psi_b = moved(psi_a, "c", C, 1)
    target = (dest_index[0, 0, :, 0] * sectors + dest_slot[0, 0])[None]
    tags = [target] + [moved(target, "x", X, by) for by in (1, 2, -1)]
    tags = jnp.concatenate(tags, axis=1).astype(BF16)
    tags = jnp.pad(tags, ((0, TAG_ROWS - 1), (0, width - tags.shape[1])))
    left = left_env.reshape(terms, shards, rows, width).transpose(1, 0, 2, 3)
    packet = jnp.concatenate(
        [
            left.reshape(shards, terms * rows, width),
            jnp.broadcast_to(tags[None], (shards, TAG_ROWS, width)),
        ],
        axis=1,
    )
    packet = lax.all_to_all(packet, MPO, split_axis=0, concat_axis=0, tiled=True)
    tags = packet[:, terms * rows, : X * terms * sectors].astype(jnp.int32)
    own, behind, far, ahead = (
        tags.reshape(shards, X, terms, sectors)[:, i] for i in range(X)
    )
    first = core == 0
    tags = jnp.concatenate(
        [
            own,
            jnp.where(first, behind, ahead),
            jnp.where(first, far[..., :part], far[..., part:]),
            jnp.where(first, ahead, behind),
            jnp.where(first, far[..., part:], far[..., :part]),
        ],
        axis=2,
    ).reshape(shards, terms * X * sectors)
    count = Z * sectors
    pairs, slots = ending_here(tags, x * count, count, X * Z * CAP)
    held = [halves(packet, p, shards * terms, rows) for p in (psi_blocks, psi_a, psi_b)]
    partial = sums(pairs, slots, held, rights, shards, count)
    partial = partial.reshape(Z, sectors, rows, width)
    partial = lax.all_to_all(partial, "z", split_axis=0, concat_axis=0, tiled=True)
    return added(partial)


def solution(mesh):
    chips = Mesh(mesh.devices.reshape(X, Z, Y, C), (*SEC, *MPO))
    in_specs = (
        P(SEC, None, None),
        P(MPO, None, None),
        P(MPO, None, None),
        P(MPO, SEC, None, None),
        P(MPO, SEC, None),
    )
    out_specs = P(SEC, MPO, None)
    return jax.shard_map(
        on_device, mesh=chips, in_specs=in_specs, out_specs=out_specs, check_vma=False
    )
```

```python
import jax
import jax.numpy as jnp
from jax import lax
from jax.experimental import pallas as pl
from jax.experimental.pallas import tpu as pltpu
from jax.sharding import Mesh
from jax.sharding import PartitionSpec as P

XB, XA, Z, Y, C = 2, 2, 8, 8, 2
X = XB * XA
AXIS_X, SEC, MPO = ("xb", "xa"), ("xb", "xa", "z"), ("y", "c")
BF16, F32 = jnp.bfloat16, jnp.float32
TAG_ROWS = 16


def half_kernel(packet_ref, psi_ref, *refs):
    half_ref = refs[-1]
    shards, _, width = packet_ref.shape
    terms, _, rows, _ = half_ref.shape
    lefts = packet_ref[:, : terms // shards * rows, :].reshape(terms * rows, width)
    out = jnp.dot(lefts, psi_ref[0], preferred_element_type=F32).astype(BF16)
    half_ref[:, 0] = out.reshape(terms, rows, width)


def halves(packet, psi, into, at, shape):
    terms, _, rows, width = shape
    count = psi.shape[0]
    before = [] if into is None else [into]
    return pl.pallas_call(
        half_kernel,
        grid=(count,),
        in_specs=[
            pl.BlockSpec(packet.shape, lambda s: (0, 0, 0)),
            pl.BlockSpec((1, width, width), lambda s: (s, 0, 0)),
        ]
        + [pl.BlockSpec(memory_space=pl.ANY) for _ in before],
        out_specs=pl.BlockSpec((terms, 1, rows, width), lambda s: (0, s + at, 0, 0)),
        out_shape=jax.ShapeDtypeStruct(shape, BF16),
        input_output_aliases={2: 0} if before else {},
        compiler_params=pltpu.CompilerParams(vmem_limit_bytes=56 << 20),
        cost_estimate=pl.CostEstimate(
            flops=2 * terms * rows * width * width * count,
            bytes_accessed=2 * count * width * (width + terms * rows),
            transcendentals=0,
        ),
        name="halves",
    )(packet, psi, *before)


def sums_kernel(place_ref, tag_ref, half_ref, right_ref, out_ref, total_ref):
    step = pl.program_id(0)
    terms, sectors, rows, width = half_ref.shape
    xb, core = place_ref[0], place_ref[1]
    count = out_ref.shape[0]
    each = sectors // X
    part = each // C
    near, away = 1 + 2 * core, 3 - 2 * core
    runs = (
        (each, 0, 0),
        (each, near, 0),
        (part, 2, core * part),
        (each, away, 0),
        (part, 2, (1 - core) * part),
    )

    @pl.when(step == 0)
    def _():
        total_ref[...] = jnp.zeros_like(total_ref)

    for w in range(terms):
        lhs = half_ref[w].reshape(sectors * rows, width)
        full = jnp.dot(lhs, right_ref[w], preferred_element_type=F32).astype(BF16)
        full = full.astype(F32).reshape(sectors, rows, width)
        s = 0
        for length, shard, first in runs:
            for k in range(length):
                t = tag_ref[step, (shard * terms + w) * each + first + k] - xb * count
                total_ref[jnp.where((t >= 0) & (t < count), t, count)] += full[s]
                s += 1

    @pl.when(step == pl.num_programs(0) - 1)
    def _():
        out_ref[...] = total_ref[:count].astype(BF16)


def sums(place, tags, half, rights, count):
    terms, sectors, rows, width = half.shape
    steps = tags.shape[0]
    each = terms // steps
    return pl.pallas_call(
        sums_kernel,
        grid_spec=pltpu.PrefetchScalarGridSpec(
            num_scalar_prefetch=2,
            grid=(steps,),
            in_specs=[
                pl.BlockSpec((each, sectors, rows, width), lambda i, *_: (i, 0, 0, 0)),
                pl.BlockSpec((each, width, width), lambda i, *_: (i, 0, 0)),
            ],
            out_specs=pl.BlockSpec((count, rows, width), lambda i, *_: (0, 0, 0)),
            scratch_shapes=[pltpu.VMEM((count + 1, rows, width), F32)],
        ),
        out_shape=jax.ShapeDtypeStruct((count, rows, width), BF16),
        compiler_params=pltpu.CompilerParams(vmem_limit_bytes=56 << 20),
        cost_estimate=pl.CostEstimate(
            flops=2 * terms * sectors * rows * width * width,
            bytes_accessed=2 * terms * width * (sectors * rows + width),
            transcendentals=0,
        ),
        name="sums",
    )(place, tags, half, rights)


def moved(block, axis, size, by):
    return lax.ppermute(block, axis, [(i, (i + by) % size) for i in range(size)])


def both_ways(block, by):
    pairs = []
    for i in range(X):
        pairs.append((i * C, (i + by) % X * C))
        pairs.append((i * C + 1, (i - by) % X * C + 1))
    return lax.ppermute(block, (*AXIS_X, "c"), pairs)


def added(parts):
    total = parts[0].astype(F32)
    for i in range(1, parts.shape[0]):
        total = total + parts[i].astype(F32)
    return total


def on_device(psi_blocks, left_env, right_env, dest_index, dest_slot):
    sectors, width = psi_blocks.shape[:2]
    terms = left_env.shape[0] // XA
    shards = Y * C
    rows = width // shards
    part = sectors // C
    xb, xa, core = lax.axis_index("xb"), lax.axis_index("xa"), lax.axis_index("c")
    right = lax.dynamic_slice_in_dim(right_env, xa * terms, terms, 0)
    rights = lax.all_gather(right, MPO, axis=0, tiled=True)
    psi_next = both_ways(psi_blocks, 1)
    psi_far = both_ways(lax.dynamic_slice_in_dim(psi_blocks, core * part, part, 0), 2)
    psi_a = jnp.concatenate([psi_next, psi_far])
    psi_b = moved(psi_a, "c", C, 1)
    target = (dest_index[0, 0, :, 0] * sectors + dest_slot[0, 0])[None]
    same = lax.dynamic_slice_in_dim(target, xa * terms * sectors, terms * sectors, 1)
    other = lax.dynamic_slice_in_dim(target, (1 - xa) * terms * sectors, terms * sectors, 1)
    tags = [
        same,
        moved(other, AXIS_X, X, 1),
        moved(same, AXIS_X, X, 2),
        moved(other, AXIS_X, X, -1),
    ]
    tags = jnp.concatenate(tags, axis=1).astype(BF16)
    tags = jnp.pad(tags, ((0, TAG_ROWS - 1), (0, width - tags.shape[1])))
    left = lax.dynamic_slice_in_dim(left_env, xa * terms, terms, 0)
    left = left.reshape(terms, shards, rows, width).transpose(1, 0, 2, 3)
    packet = jnp.concatenate(
        [
            left.reshape(shards, terms * rows, width),
            jnp.broadcast_to(tags[None], (shards, TAG_ROWS, width)),
        ],
        axis=1,
    )
    packet = lax.all_to_all(packet, MPO, split_axis=0, concat_axis=0, tiled=True)
    tags = packet[:, terms * rows, : X * terms * sectors].astype(jnp.int32)
    place = jnp.stack([xb, core]).astype(jnp.int32)
    count = XA * Z * sectors
    shape = (shards * terms, X * sectors, rows, width)
    half, at = None, 0
    for psi in (psi_blocks, psi_a, psi_b):
        half = halves(packet, psi, half, at, shape)
        at += psi.shape[0]
    partial = sums(place, tags, half, rights, count)
    partial = partial.reshape(XA * Z, sectors, rows, width)
    partial = lax.all_to_all(partial, ("xa", "z"), split_axis=0, concat_axis=0, tiled=True)
    return added(partial)


def solution(mesh):
    chips = Mesh(mesh.devices.reshape(XB, XA, Z, Y, C), (*SEC, *MPO))
    in_specs = (
        P(SEC, None, None),
        P(MPO, None, None),
        P(MPO, None, None),
        P(MPO, SEC, None, None),
        P(MPO, SEC, None),
    )
    out_specs = P(SEC, MPO, None)
    return jax.shard_map(
        on_device, mesh=chips, in_specs=in_specs, out_specs=out_specs, check_vma=False
    )
```

```python
import jax
import jax.numpy as jnp
from jax import lax
from jax.experimental import pallas as pl
from jax.experimental.pallas import tpu as pltpu
from jax.sharding import Mesh
from jax.sharding import PartitionSpec as P

XB, XA, Z, Y, C = 2, 2, 8, 8, 2
X = XB * XA
AXIS_X, SEC, MPO = ("xb", "xa"), ("xb", "xa", "z"), ("y", "c")
BF16, F32 = jnp.bfloat16, jnp.float32
TAG_ROWS = 16
STEPS = 4


def half_kernel(packet_ref, *refs):
    half_ref = refs[-1]
    shards, _, width = packet_ref.shape
    terms, _, rows, _ = half_ref.shape
    lefts = packet_ref[:, : terms // shards * rows, :].reshape(terms * rows, width)
    at = 0
    for psi_ref in refs[:-1]:
        for k in range(psi_ref.shape[0]):
            out = jnp.dot(lefts, psi_ref[k], preferred_element_type=F32).astype(BF16)
            half_ref[:, at] = out.reshape(terms, rows, width)
            at += 1


def halves(packet, pieces, terms, rows):
    count = sum(p.shape[0] for p in pieces)
    width = packet.shape[2]
    return pl.pallas_call(
        half_kernel,
        out_shape=jax.ShapeDtypeStruct((terms, count, rows, width), BF16),
        compiler_params=pltpu.CompilerParams(vmem_limit_bytes=32 << 20),
        cost_estimate=pl.CostEstimate(
            flops=2 * terms * rows * width * width * count,
            bytes_accessed=2 * count * width * (width + terms * rows),
            transcendentals=0,
        ),
        name="halves",
    )(packet, *pieces)


def sums_kernel(place_ref, tag_ref, half_a, half_b, right_ref, out_ref, *total_refs):
    step = pl.program_id(0)
    terms, sectors_a, rows, width = half_a.shape
    sectors_b = half_b.shape[1]
    xb, core = place_ref[0], place_ref[1]
    count = out_ref.shape[0]
    each = (sectors_a + sectors_b) // X
    part = each // C
    near, away = 1 + 2 * core, 3 - 2 * core
    runs = (
        ((each, 0, 0), (each, near, 0), (part, 2, core * part)),
        ((each, away, 0), (part, 2, (1 - core) * part)),
    )
    own = tag_ref.shape[1] // (X * each)

    @pl.when(step == 0)
    def _():
        for total_ref in total_refs:
            total_ref[...] = jnp.zeros_like(total_ref)

    turn = 0
    for w in range(terms):
        row = step * (terms // own) + w // own
        for half_ref, some in zip((half_a, half_b), runs, strict=True):
            number = half_ref.shape[1]
            lhs = half_ref[w].reshape(number * rows, width)
            full = jnp.dot(lhs, right_ref[w], preferred_element_type=F32).astype(BF16)
            full = full.astype(F32).reshape(number, rows, width)
            s = 0
            for length, shard, first in some:
                for k in range(length):
                    t = tag_ref[row, (shard * own + w % own) * each + first + k] - xb * count
                    t = jnp.where((t >= 0) & (t < count), t, count)
                    total_ref = total_refs[turn % len(total_refs)]
                    total_ref[t] += full[s]
                    s += 1
                    turn += 1

    @pl.when(step == pl.num_programs(0) - 1)
    def _():
        total = total_refs[0][:count]
        for total_ref in total_refs[1:]:
            total = total + total_ref[:count]
        out_ref[...] = total.astype(BF16)


def sums(place, tags, half_a, half_b, rights, count, steps):
    terms, _, rows, width = half_a.shape
    each = terms // steps
    pairs = terms * (half_a.shape[1] + half_b.shape[1])
    return pl.pallas_call(
        sums_kernel,
        grid_spec=pltpu.PrefetchScalarGridSpec(
            num_scalar_prefetch=2,
            grid=(steps,),
            in_specs=[
                pl.BlockSpec((each, h.shape[1], rows, width), lambda i, *_: (i, 0, 0, 0))
                for h in (half_a, half_b)
            ]
            + [pl.BlockSpec((each, width, width), lambda i, *_: (i, 0, 0))],
            out_specs=pl.BlockSpec((count, rows, width), lambda i, *_: (0, 0, 0)),
            scratch_shapes=[pltpu.VMEM((count + 1, rows, width), F32)] * 2,
        ),
        out_shape=jax.ShapeDtypeStruct((count, rows, width), BF16),
        compiler_params=pltpu.CompilerParams(vmem_limit_bytes=56 << 20),
        cost_estimate=pl.CostEstimate(
            flops=2 * pairs * rows * width * width,
            bytes_accessed=2 * width * (pairs * rows + terms * width),
            transcendentals=0,
        ),
        name="sums",
    )(place, tags, half_a, half_b, rights)


def moved(block, axis, size, by):
    return lax.ppermute(block, axis, [(i, (i + by) % size) for i in range(size)])


def both_ways(block, by):
    pairs = []
    for i in range(X):
        pairs.append((i * C, (i + by) % X * C))
        pairs.append((i * C + 1, (i - by) % X * C + 1))
    return lax.ppermute(block, (*AXIS_X, "c"), pairs)


def added(parts):
    total = parts[0].astype(F32)
    for i in range(1, parts.shape[0]):
        total = total + parts[i].astype(F32)
    return total


def on_device(psi_blocks, left_env, right_env, dest_index, dest_slot):
    sectors, width = psi_blocks.shape[:2]
    terms = left_env.shape[0] // XA
    shards = Y * C
    rows = width // shards
    part = sectors // C
    xb, xa, core = lax.axis_index("xb"), lax.axis_index("xa"), lax.axis_index("c")
    right = lax.dynamic_slice_in_dim(right_env, xa * terms, terms, 0)
    rights = lax.all_gather(right, MPO, axis=0, tiled=True)
    psi_next = both_ways(psi_blocks, 1)
    psi_far = both_ways(lax.dynamic_slice_in_dim(psi_blocks, core * part, part, 0), 2)
    target = (dest_index[0, 0, :, 0] * sectors + dest_slot[0, 0])[None]
    same = lax.dynamic_slice_in_dim(target, xa * terms * sectors, terms * sectors, 1)
    other = lax.dynamic_slice_in_dim(target, (1 - xa) * terms * sectors, terms * sectors, 1)
    tags = [
        same,
        moved(other, AXIS_X, X, 1),
        moved(same, AXIS_X, X, 2),
        moved(other, AXIS_X, X, -1),
    ]
    tags = jnp.concatenate(tags, axis=1).astype(BF16)
    tags = jnp.pad(tags, ((0, TAG_ROWS - 1), (0, width - tags.shape[1])))
    left = lax.dynamic_slice_in_dim(left_env, xa * terms, terms, 0)
    left = left.reshape(terms, shards, rows, width).transpose(1, 0, 2, 3)
    packet = jnp.concatenate(
        [
            left.reshape(shards, terms * rows, width),
            jnp.broadcast_to(tags[None], (shards, TAG_ROWS, width)),
        ],
        axis=1,
    )
    psi_next, psi_far, _ = lax.optimization_barrier((psi_next, psi_far, packet))
    packet = lax.all_to_all(packet, MPO, split_axis=0, concat_axis=0, tiled=True)
    tags = packet[:, terms * rows, : X * terms * sectors].astype(jnp.int32)
    place = jnp.stack([xb, core]).astype(jnp.int32)
    half_a = halves(packet, [psi_blocks, psi_next, psi_far], shards * terms, rows)
    theirs = [moved(psi_next, "c", C, 1), moved(psi_far, "c", C, 1)]
    half_b = halves(packet, theirs, shards * terms, rows)
    partial = sums(place, tags, half_a, half_b, rights, XA * Z * sectors, STEPS)
    partial = partial.reshape(XA * Z, sectors, rows, width)
    partial = lax.all_to_all(partial, ("xa", "z"), split_axis=0, concat_axis=0, tiled=True)
    return added(partial)


def solution(mesh):
    chips = Mesh(mesh.devices.reshape(XB, XA, Z, Y, C), (*SEC, *MPO))
    in_specs = (
        P(SEC, None, None),
        P(MPO, None, None),
        P(MPO, None, None),
        P(MPO, SEC, None, None),
        P(MPO, SEC, None),
    )
    out_specs = P(SEC, MPO, None)
    return jax.shard_map(
        on_device, mesh=chips, in_specs=in_specs, out_specs=out_specs, check_vma=False
    )
```

```python
import jax
import jax.numpy as jnp
from jax import lax
from jax.experimental import pallas as pl
from jax.experimental.pallas import tpu as pltpu
from jax.sharding import Mesh
from jax.sharding import PartitionSpec as P

XB, XA, Z, Y, C = 2, 2, 8, 8, 2
X = XB * XA
AXIS_X, SEC, MPO = ("xb", "xa"), ("xb", "xa", "z"), ("y", "c")
BF16, F32 = jnp.bfloat16, jnp.float32
TAG_ROWS = 16
STEPS = 4


def half_kernel(packet_ref, *refs):
    half_ref = refs[-1]
    shards, _, width = packet_ref.shape
    terms, _, rows, _ = half_ref.shape
    lefts = packet_ref[:, : terms // shards * rows, :].reshape(terms * rows, width)
    at = 0
    for psi_ref in refs[:-1]:
        for k in range(psi_ref.shape[0]):
            out = jnp.dot(lefts, psi_ref[k], preferred_element_type=F32).astype(BF16)
            half_ref[:, at] = out.reshape(terms, rows, width)
            at += 1


def halves(packet, pieces, terms, rows):
    count = sum(p.shape[0] for p in pieces)
    width = packet.shape[2]
    return pl.pallas_call(
        half_kernel,
        out_shape=jax.ShapeDtypeStruct((terms, count, rows, width), BF16),
        compiler_params=pltpu.CompilerParams(vmem_limit_bytes=16 << 20),
        cost_estimate=pl.CostEstimate(
            flops=2 * terms * rows * width * width * count,
            bytes_accessed=2 * count * width * (width + terms * rows),
            transcendentals=0,
        ),
        name="halves",
    )(packet, *pieces)


def sums_kernel(place_ref, tag_ref, half_a, half_b, right_ref, out_ref, *total_refs):
    step = pl.program_id(0)
    terms, sectors_a, rows, width = half_a.shape
    sectors_b = half_b.shape[1]
    xb, core = place_ref[0], place_ref[1]
    count = out_ref.shape[0]
    each = (sectors_a + sectors_b) // X
    part = each // C
    near, away = 1 + 2 * core, 3 - 2 * core
    runs = (
        ((each, 0, 0), (each, near, 0), (part, 2, core * part)),
        ((each, away, 0), (part, 2, (1 - core) * part)),
    )
    own = tag_ref.shape[1] // (X * each)

    @pl.when(step == 0)
    def _():
        for total_ref in total_refs:
            total_ref[...] = jnp.zeros_like(total_ref)

    turn = 0
    for w in range(terms):
        row = step * (terms // own) + w // own
        for half_ref, some in zip((half_a, half_b), runs, strict=True):
            number = half_ref.shape[1]
            lhs = half_ref[w].reshape(number * rows, width)
            full = jnp.dot(lhs, right_ref[w], preferred_element_type=F32).astype(BF16)
            full = full.astype(F32).reshape(number, rows, width)
            s = 0
            for length, shard, first in some:
                for k in range(length):
                    t = tag_ref[row, (shard * own + w % own) * each + first + k] - xb * count
                    t = jnp.where((t >= 0) & (t < count), t, count)
                    total_ref = total_refs[turn % len(total_refs)]
                    total_ref[t] += full[s]
                    s += 1
                    turn += 1

    @pl.when(step == pl.num_programs(0) - 1)
    def _():
        total = total_refs[0][:count]
        for total_ref in total_refs[1:]:
            total = total + total_ref[:count]
        out_ref[...] = total.astype(BF16)


def sums(place, tags, half_a, half_b, rights, count, steps):
    terms, _, rows, width = half_a.shape
    each = terms // steps
    pairs = terms * (half_a.shape[1] + half_b.shape[1])
    return pl.pallas_call(
        sums_kernel,
        grid_spec=pltpu.PrefetchScalarGridSpec(
            num_scalar_prefetch=2,
            grid=(steps,),
            in_specs=[
                pl.BlockSpec((each, h.shape[1], rows, width), lambda i, *_: (i, 0, 0, 0))
                for h in (half_a, half_b)
            ]
            + [pl.BlockSpec((each, width, width), lambda i, *_: (i, 0, 0))],
            out_specs=pl.BlockSpec((count, rows, width), lambda i, *_: (0, 0, 0)),
            scratch_shapes=[pltpu.VMEM((count + 1, rows, width), F32)] * 2,
        ),
        out_shape=jax.ShapeDtypeStruct((count, rows, width), BF16),
        compiler_params=pltpu.CompilerParams(vmem_limit_bytes=56 << 20),
        cost_estimate=pl.CostEstimate(
            flops=2 * pairs * rows * width * width,
            bytes_accessed=2 * width * (pairs * rows + terms * width),
            transcendentals=0,
        ),
        name="sums",
    )(place, tags, half_a, half_b, rights)


def moved(block, axis, size, by):
    return lax.ppermute(block, axis, [(i, (i + by) % size) for i in range(size)])


def both_ways(block, by):
    pairs = []
    for i in range(X):
        pairs.append((i * C, (i + by) % X * C))
        pairs.append((i * C + 1, (i - by) % X * C + 1))
    return lax.ppermute(block, (*AXIS_X, "c"), pairs)


def added(parts):
    total = parts[0].astype(F32)
    for i in range(1, parts.shape[0]):
        total = total + parts[i].astype(F32)
    return total


def on_device(psi_blocks, left_env, right_env, dest_index, dest_slot):
    sectors, width = psi_blocks.shape[:2]
    terms = left_env.shape[0] // XA
    shards = Y * C
    rows = width // shards
    part = sectors // C
    xb, xa, core = lax.axis_index("xb"), lax.axis_index("xa"), lax.axis_index("c")
    right = lax.dynamic_slice_in_dim(right_env, xa * terms, terms, 0)
    rights = lax.all_gather(right, MPO, axis=0, tiled=True)
    target = (dest_index[0, 0, :, 0] * sectors + dest_slot[0, 0])[None]
    same = lax.dynamic_slice_in_dim(target, xa * terms * sectors, terms * sectors, 1)
    other = lax.dynamic_slice_in_dim(target, (1 - xa) * terms * sectors, terms * sectors, 1)
    tags = [
        same,
        moved(other, AXIS_X, X, 1),
        moved(same, AXIS_X, X, 2),
        moved(other, AXIS_X, X, -1),
    ]
    tags = jnp.concatenate(tags, axis=1).astype(BF16)
    tags = jnp.pad(tags, ((0, TAG_ROWS - 1), (0, width - tags.shape[1])))
    sent, _ = lax.optimization_barrier((psi_blocks, tags))
    psi_next = both_ways(sent, 1)
    psi_far = both_ways(lax.dynamic_slice_in_dim(sent, core * part, part, 0), 2)
    left = lax.dynamic_slice_in_dim(left_env, xa * terms, terms, 0)
    left = left.reshape(terms, shards, rows, width).transpose(1, 0, 2, 3)
    packet = jnp.concatenate(
        [
            left.reshape(shards, terms * rows, width),
            jnp.broadcast_to(tags[None], (shards, TAG_ROWS, width)),
        ],
        axis=1,
    )
    psi_next, psi_far, _ = lax.optimization_barrier((psi_next, psi_far, packet))
    packet = lax.all_to_all(packet, MPO, split_axis=0, concat_axis=0, tiled=True)
    tags = packet[:, terms * rows, : X * terms * sectors].astype(jnp.int32)
    place = jnp.stack([xb, core]).astype(jnp.int32)
    half_a = halves(packet, [psi_blocks, psi_next, psi_far], shards * terms, rows)
    theirs = [moved(psi_next, "c", C, 1), moved(psi_far, "c", C, 1)]
    half_b = halves(packet, theirs, shards * terms, rows)
    partial = sums(place, tags, half_a, half_b, rights, XA * Z * sectors, STEPS)
    partial = partial.reshape(XA * Z, sectors, rows, width)
    partial = lax.all_to_all(partial, ("xa", "z"), split_axis=0, concat_axis=0, tiled=True)
    return added(partial)


def solution(mesh):
    chips = Mesh(mesh.devices.reshape(XB, XA, Z, Y, C), (*SEC, *MPO))
    in_specs = (
        P(SEC, None, None),
        P(MPO, None, None),
        P(MPO, None, None),
        P(MPO, SEC, None, None),
        P(MPO, SEC, None),
    )
    out_specs = P(SEC, MPO, None)
    return jax.shard_map(
        on_device, mesh=chips, in_specs=in_specs, out_specs=out_specs, check_vma=False
    )
```

```python
import jax
import jax.numpy as jnp
from jax import lax
from jax.experimental import pallas as pl
from jax.experimental.pallas import tpu as pltpu
from jax.sharding import Mesh
from jax.sharding import PartitionSpec as P

XB, XA, Z, Y, C = 2, 2, 8, 8, 2
X = XB * XA
AXIS_X, SEC, MPO = ("xb", "xa"), ("xb", "xa", "z"), ("y", "c")
BF16, F32 = jnp.bfloat16, jnp.float32
TAG_ROWS = 8
STEPS = 2


def half_kernel(packet_ref, *refs):
    half_ref = refs[-1]
    shards, _, width = packet_ref.shape
    terms, _, rows, _ = half_ref.shape
    lefts = packet_ref[:, : terms // shards * rows, :].reshape(terms * rows, width)
    at = 0
    for psi_ref in refs[:-1]:
        for k in range(psi_ref.shape[0]):
            out = jnp.dot(lefts, psi_ref[k], preferred_element_type=F32).astype(BF16)
            half_ref[:, at] = out.reshape(terms, rows, width)
            at += 1


def halves(packet, pieces, terms, rows):
    count = sum(p.shape[0] for p in pieces)
    width = packet.shape[2]
    return pl.pallas_call(
        half_kernel,
        out_shape=jax.ShapeDtypeStruct((terms, count, rows, width), BF16),
        compiler_params=pltpu.CompilerParams(vmem_limit_bytes=16 << 20),
        cost_estimate=pl.CostEstimate(
            flops=2 * terms * rows * width * width * count,
            bytes_accessed=2 * count * width * (width + terms * rows),
            transcendentals=0,
        ),
        name="halves",
    )(packet, *pieces)


def sums_kernel(place_ref, tag_ref, half_a, half_b, right_ref, out_ref, *total_refs):
    step = pl.program_id(0)
    terms, sectors_a, rows, width = half_a.shape
    sectors_b = half_b.shape[1]
    xb, core = place_ref[0], place_ref[1]
    count = out_ref.shape[0]
    each = (sectors_a + sectors_b) // X
    part = each // C
    near, away = 1 + 2 * core, 3 - 2 * core
    runs = (
        ((each, 0, 0), (each, near, 0)),
        ((part, 2, core * part), (each, away, 0), (part, 2, (1 - core) * part)),
    )
    own = tag_ref.shape[1] // (X * each)

    @pl.when(step == 0)
    def _():
        for total_ref in total_refs:
            total_ref[...] = jnp.zeros_like(total_ref)

    turn = 0
    for w in range(terms):
        row = step * (terms // own) + w // own
        for half_ref, some in zip((half_a, half_b), runs, strict=True):
            number = half_ref.shape[1]
            lhs = half_ref[w].reshape(number * rows, width)
            full = jnp.dot(lhs, right_ref[w], preferred_element_type=F32).astype(BF16)
            full = full.astype(F32).reshape(number, rows, width)
            s = 0
            for length, shard, first in some:
                for k in range(length):
                    t = tag_ref[row, (shard * own + w % own) * each + first + k] - xb * count
                    t = jnp.where((t >= 0) & (t < count), t, count)
                    total_ref = total_refs[turn % len(total_refs)]
                    total_ref[t] += full[s]
                    s += 1
                    turn += 1

    @pl.when(step == pl.num_programs(0) - 1)
    def _():
        total = total_refs[0][:count]
        for total_ref in total_refs[1:]:
            total = total + total_ref[:count]
        out_ref[...] = total.astype(BF16)


def sums(place, tags, half_a, half_b, rights, count, steps):
    terms, _, rows, width = half_a.shape
    each = terms // steps
    pairs = terms * (half_a.shape[1] + half_b.shape[1])
    return pl.pallas_call(
        sums_kernel,
        grid_spec=pltpu.PrefetchScalarGridSpec(
            num_scalar_prefetch=2,
            grid=(steps,),
            in_specs=[
                pl.BlockSpec((each, h.shape[1], rows, width), lambda i, *_: (i, 0, 0, 0))
                for h in (half_a, half_b)
            ]
            + [pl.BlockSpec((each, width, width), lambda i, *_: (i, 0, 0))],
            out_specs=pl.BlockSpec((count, rows, width), lambda i, *_: (0, 0, 0)),
            scratch_shapes=[pltpu.VMEM((count + 1, rows, width), F32)] * 2,
        ),
        out_shape=jax.ShapeDtypeStruct((count, rows, width), BF16),
        compiler_params=pltpu.CompilerParams(vmem_limit_bytes=56 << 20),
        cost_estimate=pl.CostEstimate(
            flops=2 * pairs * rows * width * width,
            bytes_accessed=2 * width * (pairs * rows + terms * width),
            transcendentals=0,
        ),
        name="sums",
    )(place, tags, half_a, half_b, rights)


def moved(block, axis, size, by):
    return lax.ppermute(block, axis, [(i, (i + by) % size) for i in range(size)])


def both_ways(block, by):
    pairs = []
    for i in range(X):
        pairs.append((i * C, (i + by) % X * C))
        pairs.append((i * C + 1, (i - by) % X * C + 1))
    return lax.ppermute(block, (*AXIS_X, "c"), pairs)


def added(parts):
    total = parts[0].astype(F32)
    for i in range(1, parts.shape[0]):
        total = total + parts[i].astype(F32)
    return total


def on_device(psi_blocks, left_env, right_env, dest_index, dest_slot):
    sectors, width = psi_blocks.shape[:2]
    terms = left_env.shape[0] // XA
    shards = Y * C
    rows = width // shards
    part = sectors // C
    xb, xa, core = lax.axis_index("xb"), lax.axis_index("xa"), lax.axis_index("c")
    right = lax.dynamic_slice_in_dim(right_env, xa * terms, terms, 0)
    rights = lax.all_gather(right, MPO, axis=0, tiled=True)
    target = (dest_index[0, 0, :, 0] * sectors + dest_slot[0, 0])[None]
    same = lax.dynamic_slice_in_dim(target, xa * terms * sectors, terms * sectors, 1)
    other = lax.dynamic_slice_in_dim(target, (1 - xa) * terms * sectors, terms * sectors, 1)
    tags = [
        same,
        moved(other, AXIS_X, X, 1),
        moved(same, AXIS_X, X, 2),
        moved(other, AXIS_X, X, -1),
    ]
    tags = jnp.concatenate(tags, axis=1).astype(BF16)
    tags = jnp.pad(tags, ((0, TAG_ROWS - 1), (0, width - tags.shape[1])))
    psi_next = both_ways(psi_blocks, 1)
    left = lax.dynamic_slice_in_dim(left_env, xa * terms, terms, 0)
    left = left.reshape(terms, shards, rows, width).transpose(1, 0, 2, 3)
    packet = jnp.concatenate(
        [
            left.reshape(shards, terms * rows, width),
            jnp.broadcast_to(tags[None], (shards, TAG_ROWS, width)),
        ],
        axis=1,
    )
    psi_next, _ = lax.optimization_barrier((psi_next, packet))
    psi_far = both_ways(lax.dynamic_slice_in_dim(psi_next, core * part, part, 0), 1)
    packet = lax.all_to_all(packet, MPO, split_axis=0, concat_axis=0, tiled=True)
    tags = packet[:, terms * rows, : X * terms * sectors].astype(jnp.int32)
    place = jnp.stack([xb, core]).astype(jnp.int32)
    half_a = halves(packet, [psi_blocks, psi_next], shards * terms, rows)
    rest = [psi_far, moved(psi_next, "c", C, 1), moved(psi_far, "c", C, 1)]
    half_b = halves(packet, rest, shards * terms, rows)
    partial = sums(place, tags, half_a, half_b, rights, XA * Z * sectors, STEPS)
    partial = partial.reshape(XA * Z, sectors, rows, width)
    partial = lax.all_to_all(partial, ("xa", "z"), split_axis=0, concat_axis=0, tiled=True)
    return added(partial)


def solution(mesh):
    chips = Mesh(mesh.devices.reshape(XB, XA, Z, Y, C), (*SEC, *MPO))
    in_specs = (
        P(SEC, None, None),
        P(MPO, None, None),
        P(MPO, None, None),
        P(MPO, SEC, None, None),
        P(MPO, SEC, None),
    )
    out_specs = P(SEC, MPO, None)
    return jax.shard_map(
        on_device, mesh=chips, in_specs=in_specs, out_specs=out_specs, check_vma=False
    )
```

```python
import jax
import jax.numpy as jnp
from jax import lax
from jax.experimental import pallas as pl
from jax.experimental.pallas import tpu as pltpu
from jax.sharding import Mesh
from jax.sharding import PartitionSpec as P

XB, XA, Z, Y, C = 2, 2, 8, 8, 2
X = XB * XA
AXIS_X, SEC, MPO = ("xb", "xa"), ("xb", "xa", "z"), ("y", "c")
BF16, F32 = jnp.bfloat16, jnp.float32
STEPS = 2


def half_kernel(left_ref, *refs):
    half_ref = refs[-1]
    terms, _, rows, width = half_ref.shape
    lefts = left_ref[...]
    at = 0
    for psi_ref in refs[:-1]:
        for k in range(psi_ref.shape[0]):
            out = jnp.dot(lefts, psi_ref[k], preferred_element_type=F32).astype(BF16)
            half_ref[:, at] = out.reshape(terms, rows, width)
            at += 1


def halves(lefts, pieces, terms):
    count = sum(p.shape[0] for p in pieces)
    width = lefts.shape[1]
    rows = lefts.shape[0] // terms
    return pl.pallas_call(
        half_kernel,
        out_shape=jax.ShapeDtypeStruct((terms, count, rows, width), BF16),
        compiler_params=pltpu.CompilerParams(vmem_limit_bytes=16 << 20),
        cost_estimate=pl.CostEstimate(
            flops=2 * terms * rows * width * width * count,
            bytes_accessed=2 * count * width * (width + terms * rows),
            transcendentals=0,
        ),
        name="halves",
    )(lefts, *pieces)


def sums_kernel(place_ref, tag_ref, half_a, half_b, right_ref, out_ref, *total_refs):
    step = pl.program_id(0)
    terms, sectors_a, rows, width = half_a.shape
    sectors_b = half_b.shape[1]
    x, core = place_ref[0], place_ref[1]
    xb = x // XA
    count = out_ref.shape[0]
    each = (sectors_a + sectors_b) // X
    part = each // C
    near, far, away = (x + X - 1 + 2 * core) % X, (x + 2) % X, (x + 1 + 2 * core) % X
    runs = (
        ((each, x, 0), (each, near, 0)),
        ((part, far, core * part), (each, away, 0), (part, far, (1 - core) * part)),
    )
    own = tag_ref.shape[1] // each
    shards = tag_ref.shape[0] // X

    @pl.when(step == 0)
    def _():
        for total_ref in total_refs:
            total_ref[...] = jnp.zeros_like(total_ref)

    turn = 0
    for w in range(terms):
        row = step * (terms // own) + w // own
        for half_ref, some in zip((half_a, half_b), runs, strict=True):
            number = half_ref.shape[1]
            lhs = half_ref[w].reshape(number * rows, width)
            full = jnp.dot(lhs, right_ref[w], preferred_element_type=F32).astype(BF16)
            full = full.astype(F32).reshape(number, rows, width)
            s = 0
            for length, shard, first in some:
                for k in range(length):
                    t = tag_ref[shard * shards + row, w % own * each + first + k] - xb * count
                    t = jnp.where((t >= 0) & (t < count), t, count)
                    total_ref = total_refs[turn % len(total_refs)]
                    total_ref[t] += full[s]
                    s += 1
                    turn += 1

    @pl.when(step == pl.num_programs(0) - 1)
    def _():
        total = total_refs[0][:count]
        for total_ref in total_refs[1:]:
            total = total + total_ref[:count]
        out_ref[...] = total.astype(BF16)


def sums(place, tags, half_a, half_b, rights, count, steps):
    terms, _, rows, width = half_a.shape
    each = terms // steps
    pairs = terms * (half_a.shape[1] + half_b.shape[1])
    return pl.pallas_call(
        sums_kernel,
        grid_spec=pltpu.PrefetchScalarGridSpec(
            num_scalar_prefetch=2,
            grid=(steps,),
            in_specs=[
                pl.BlockSpec((each, h.shape[1], rows, width), lambda i, *_: (i, 0, 0, 0))
                for h in (half_a, half_b)
            ]
            + [pl.BlockSpec((each, width, width), lambda i, *_: (i, 0, 0))],
            out_specs=pl.BlockSpec((count, rows, width), lambda i, *_: (0, 0, 0)),
            scratch_shapes=[pltpu.VMEM((count + 1, rows, width), F32)] * 2,
        ),
        out_shape=jax.ShapeDtypeStruct((count, rows, width), BF16),
        compiler_params=pltpu.CompilerParams(vmem_limit_bytes=56 << 20),
        cost_estimate=pl.CostEstimate(
            flops=2 * pairs * rows * width * width,
            bytes_accessed=2 * width * (pairs * rows + terms * width),
            transcendentals=0,
        ),
        name="sums",
    )(place, tags, half_a, half_b, rights)


def moved(block, axis, size, by):
    return lax.ppermute(block, axis, [(i, (i + by) % size) for i in range(size)])


def both_ways(block, by):
    pairs = []
    for i in range(X):
        pairs.append((i * C, (i + by) % X * C))
        pairs.append((i * C + 1, (i - by) % X * C + 1))
    return lax.ppermute(block, (*AXIS_X, "c"), pairs)


def added(parts):
    total = parts[0].astype(F32)
    for i in range(1, parts.shape[0]):
        total = total + parts[i].astype(F32)
    return total


def on_device(psi_blocks, left_env, right_env, dest_index, dest_slot):
    sectors, width = psi_blocks.shape[:2]
    terms = left_env.shape[0] // XA
    shards = Y * C
    rows = width // shards
    part = sectors // C
    xb, xa, core = lax.axis_index("xb"), lax.axis_index("xa"), lax.axis_index("c")
    right = lax.dynamic_slice_in_dim(right_env, xa * terms, terms, 0)
    rights = lax.all_gather(right, MPO, axis=0, tiled=True)
    left = lax.dynamic_slice_in_dim(left_env, xa * terms, terms, 0)
    left = left.reshape(terms, shards, rows, width).transpose(1, 0, 2, 3)
    left = left.reshape(shards, terms * rows, width)
    lefts = lax.all_to_all(left, MPO, split_axis=0, concat_axis=0, tiled=True)
    psi_next = both_ways(psi_blocks, 1)
    target = dest_index[0, 0, :, 0] * sectors + dest_slot[0, 0]
    lefts, psi_next, target = lax.optimization_barrier((lefts, psi_next, target))
    psi_far = both_ways(lax.dynamic_slice_in_dim(psi_next, core * part, part, 0), 1)
    target = jnp.broadcast_to(
        target.reshape(1, XA, 1, terms * sectors), (XB, XA, shards, terms * sectors)
    )
    tags = lax.all_to_all(
        target.reshape(X * shards, -1), (*AXIS_X, *MPO), split_axis=0, concat_axis=0, tiled=True
    )
    place = jnp.stack([xb * XA + xa, core]).astype(jnp.int32)
    lefts = lefts.reshape(shards * terms * rows, width)
    half_a = halves(lefts, [psi_blocks, psi_next], shards * terms)
    rest = [psi_far, moved(psi_next, "c", C, 1), moved(psi_far, "c", C, 1)]
    half_b = halves(lefts, rest, shards * terms)
    partial = sums(place, tags, half_a, half_b, rights, XA * Z * sectors, STEPS)
    partial = partial.reshape(XA * Z, sectors, rows, width)
    partial = lax.all_to_all(partial, ("xa", "z"), split_axis=0, concat_axis=0, tiled=True)
    return added(partial)


def solution(mesh):
    chips = Mesh(mesh.devices.reshape(XB, XA, Z, Y, C), (*SEC, *MPO))
    in_specs = (
        P(SEC, None, None),
        P(MPO, None, None),
        P(MPO, None, None),
        P(MPO, SEC, None, None),
        P(MPO, SEC, None),
    )
    out_specs = P(SEC, MPO, None)
    return jax.shard_map(
        on_device, mesh=chips, in_specs=in_specs, out_specs=out_specs, check_vma=False
    )
```

```python
import jax
import jax.numpy as jnp
from jax import lax
from jax.experimental import pallas as pl
from jax.experimental.pallas import tpu as pltpu
from jax.sharding import Mesh
from jax.sharding import PartitionSpec as P

XB, XA, Z, Y, C = 2, 2, 8, 8, 2
X = XB * XA
AXIS_X, SEC, MPO = ("xb", "xa"), ("xb", "xa", "z"), ("y", "c")
BF16, F32 = jnp.bfloat16, jnp.float32
STEPS = 4


def half_kernel(left_ref, *refs):
    psi_refs, (half_ref, held_ref, sems) = refs[:-3], refs[-3:]
    _, terms, rows, width = held_ref.shape
    lefts = left_ref[...]
    copies = []
    for psi_ref in psi_refs:
        for k in range(psi_ref.shape[0]):
            at = len(copies)
            out = jnp.dot(lefts, psi_ref[k], preferred_element_type=F32).astype(BF16)
            held_ref[at] = out.reshape(terms, rows, width)
            copies.append(pltpu.make_async_copy(held_ref.at[at], half_ref.at[at], sems.at[at]))
            copies[-1].start()
    for copy in copies:
        copy.wait()


def halves(lefts, pieces, terms):
    count = sum(p.shape[0] for p in pieces)
    width = lefts.shape[1]
    rows = lefts.shape[0] // terms
    return pl.pallas_call(
        half_kernel,
        in_specs=[pl.BlockSpec(memory_space=pltpu.VMEM)] * (1 + len(pieces)),
        out_specs=pl.BlockSpec(memory_space=pltpu.HBM),
        out_shape=pltpu.HBM((count, terms, rows, width), BF16),
        scratch_shapes=[
            pltpu.VMEM((count, terms, rows, width), BF16),
            pltpu.SemaphoreType.DMA((count,)),
        ],
        compiler_params=pltpu.CompilerParams(vmem_limit_bytes=16 << 20),
        cost_estimate=pl.CostEstimate(
            flops=2 * terms * rows * width * width * count,
            bytes_accessed=2 * count * width * (width + terms * rows),
            transcendentals=0,
        ),
        name="halves",
    )(lefts, *pieces)


def sums_kernel(place_ref, tag_ref, half_a, half_b, right_ref, out_ref, *total_refs):
    step = pl.program_id(0)
    sectors_a, terms, rows, width = half_a.shape
    sectors_b = half_b.shape[0]
    x, core = place_ref[0], place_ref[1]
    xb = x // XA
    count = out_ref.shape[0]
    each = (sectors_a + sectors_b) // X
    part = each // C
    near, far, away = (x + X - 1 + 2 * core) % X, (x + 2) % X, (x + 1 + 2 * core) % X
    runs = (
        ((each, x, 0), (each, near, 0)),
        ((part, far, core * part), (each, away, 0), (part, far, (1 - core) * part)),
    )
    own = tag_ref.shape[1] // each
    shards = tag_ref.shape[0] // X

    @pl.when(step == 0)
    def _():
        for total_ref in total_refs:
            total_ref[...] = jnp.zeros_like(total_ref)

    turn = 0
    for w in range(terms):
        row = step * (terms // own) + w // own
        for half_ref, some in zip((half_a, half_b), runs, strict=True):
            number = half_ref.shape[0]
            lhs = half_ref[:, w].reshape(number * rows, width)
            full = jnp.dot(lhs, right_ref[w], preferred_element_type=F32).astype(BF16)
            full = full.astype(F32).reshape(number, rows, width)
            s = 0
            for length, shard, first in some:
                for k in range(length):
                    t = tag_ref[shard * shards + row, w % own * each + first + k] - xb * count
                    t = jnp.where((t >= 0) & (t < count), t, count)
                    total_ref = total_refs[turn % len(total_refs)]
                    total_ref[t] += full[s]
                    s += 1
                    turn += 1

    @pl.when(step == pl.num_programs(0) - 1)
    def _():
        total = total_refs[0][:count]
        for total_ref in total_refs[1:]:
            total = total + total_ref[:count]
        out_ref[...] = total.astype(BF16)


def sums(place, tags, half_a, half_b, rights, count, steps):
    _, terms, rows, width = half_a.shape
    each = terms // steps
    pairs = terms * (half_a.shape[0] + half_b.shape[0])
    return pl.pallas_call(
        sums_kernel,
        grid_spec=pltpu.PrefetchScalarGridSpec(
            num_scalar_prefetch=2,
            grid=(steps,),
            in_specs=[
                pl.BlockSpec((h.shape[0], each, rows, width), lambda i, *_: (0, i, 0, 0))
                for h in (half_a, half_b)
            ]
            + [pl.BlockSpec((each, width, width), lambda i, *_: (i, 0, 0))],
            out_specs=pl.BlockSpec((count, rows, width), lambda i, *_: (0, 0, 0)),
            scratch_shapes=[pltpu.VMEM((count + 1, rows, width), F32)] * 2,
        ),
        out_shape=jax.ShapeDtypeStruct((count, rows, width), BF16),
        compiler_params=pltpu.CompilerParams(vmem_limit_bytes=56 << 20),
        cost_estimate=pl.CostEstimate(
            flops=2 * pairs * rows * width * width,
            bytes_accessed=2 * width * (pairs * rows + terms * width),
            transcendentals=0,
        ),
        name="sums",
    )(place, tags, half_a, half_b, rights)


def moved(block, axis, size, by):
    return lax.ppermute(block, axis, [(i, (i + by) % size) for i in range(size)])


def both_ways(block, by):
    pairs = []
    for i in range(X):
        pairs.append((i * C, (i + by) % X * C))
        pairs.append((i * C + 1, (i - by) % X * C + 1))
    return lax.ppermute(block, (*AXIS_X, "c"), pairs)


def added(parts):
    total = parts[0].astype(F32)
    for i in range(1, parts.shape[0]):
        total = total + parts[i].astype(F32)
    return total


def on_device(psi_blocks, left_env, right_env, dest_index, dest_slot):
    sectors, width = psi_blocks.shape[:2]
    terms = left_env.shape[0] // XA
    shards = Y * C
    rows = width // shards
    part = sectors // C
    xb, xa, core = lax.axis_index("xb"), lax.axis_index("xa"), lax.axis_index("c")
    right = lax.dynamic_slice_in_dim(right_env, xa * terms, terms, 0)
    rights = lax.all_gather(right, MPO, axis=0, tiled=True)
    left = lax.dynamic_slice_in_dim(left_env, xa * terms, terms, 0)
    left = left.reshape(terms, shards, rows, width).transpose(1, 0, 2, 3)
    left = left.reshape(shards, terms * rows, width)
    lefts = lax.all_to_all(left, MPO, split_axis=0, concat_axis=0, tiled=True)
    psi_next = both_ways(psi_blocks, 1)
    target = dest_index[0, 0, :, 0] * sectors + dest_slot[0, 0]
    lefts, psi_next, target = lax.optimization_barrier((lefts, psi_next, target))
    psi_far = both_ways(lax.dynamic_slice_in_dim(psi_next, core * part, part, 0), 1)
    target = jnp.broadcast_to(
        target.reshape(1, XA, 1, terms * sectors), (XB, XA, shards, terms * sectors)
    )
    tags = lax.all_to_all(
        target.reshape(X * shards, -1), (*AXIS_X, *MPO), split_axis=0, concat_axis=0, tiled=True
    )
    place = jnp.stack([xb * XA + xa, core]).astype(jnp.int32)
    lefts = lefts.reshape(shards * terms * rows, width)
    half_a = halves(lefts, [psi_blocks, psi_next], shards * terms)
    rest = [psi_far, moved(psi_next, "c", C, 1), moved(psi_far, "c", C, 1)]
    half_b = halves(lefts, rest, shards * terms)
    partial = sums(place, tags, half_a, half_b, rights, XA * Z * sectors, STEPS)
    partial = partial.reshape(XA * Z, sectors, rows, width)
    partial = lax.all_to_all(partial, ("xa", "z"), split_axis=0, concat_axis=0, tiled=True)
    return added(partial)


def solution(mesh):
    chips = Mesh(mesh.devices.reshape(XB, XA, Z, Y, C), (*SEC, *MPO))
    in_specs = (
        P(SEC, None, None),
        P(MPO, None, None),
        P(MPO, None, None),
        P(MPO, SEC, None, None),
        P(MPO, SEC, None),
    )
    out_specs = P(SEC, MPO, None)
    return jax.shard_map(
        on_device, mesh=chips, in_specs=in_specs, out_specs=out_specs, check_vma=False
    )
```

```python
import jax
import jax.numpy as jnp
from jax import lax
from jax.experimental import pallas as pl
from jax.experimental.pallas import tpu as pltpu
from jax.sharding import Mesh
from jax.sharding import PartitionSpec as P

XB, XA, Z, Y, C = 2, 2, 8, 8, 2
X = XB * XA
AXIS_X, SEC, MPO = ("xb", "xa"), ("xb", "xa", "z"), ("y", "c")
BF16, F32 = jnp.bfloat16, jnp.float32
STEPS = 4


def half_kernel(left_ref, *refs):
    psi_refs, (half_ref, held_ref, sems) = refs[:-3], refs[-3:]
    _, terms, rows, width = held_ref.shape
    lefts = left_ref[...]
    copies = []
    for psi_ref in psi_refs:
        for k in range(psi_ref.shape[0]):
            at = len(copies)
            out = jnp.dot(lefts, psi_ref[k], preferred_element_type=F32).astype(BF16)
            held_ref[at] = out.reshape(terms, rows, width)
            copies.append(pltpu.make_async_copy(held_ref.at[at], half_ref.at[at], sems.at[at]))
            copies[-1].start()
    for copy in copies:
        copy.wait()


def halves(lefts, pieces, terms):
    count = sum(p.shape[0] for p in pieces)
    width = lefts.shape[1]
    rows = lefts.shape[0] // terms
    return pl.pallas_call(
        half_kernel,
        in_specs=[pl.BlockSpec(memory_space=pltpu.VMEM)] * (1 + len(pieces)),
        out_specs=pl.BlockSpec(memory_space=pltpu.HBM),
        out_shape=pltpu.HBM((count, terms, rows, width), BF16),
        scratch_shapes=[
            pltpu.VMEM((count, terms, rows, width), BF16),
            pltpu.SemaphoreType.DMA((count,)),
        ],
        compiler_params=pltpu.CompilerParams(vmem_limit_bytes=16 << 20),
        cost_estimate=pl.CostEstimate(
            flops=2 * terms * rows * width * width * count,
            bytes_accessed=2 * count * width * (width + terms * rows),
            transcendentals=0,
        ),
        name="halves",
    )(lefts, *pieces)


def sums_kernel(place_ref, tag_ref, half_a, half_b, right_ref, out_ref, *total_refs):
    step = pl.program_id(0)
    sectors_a, terms, rows, width = half_a.shape
    sectors_b = half_b.shape[0]
    x, core = place_ref[0], place_ref[1]
    xb = x // XA
    count = out_ref.shape[0]
    each = (sectors_a + sectors_b) // X
    part = each // C
    near, far, away = (x + X - 1 + 2 * core) % X, (x + 2) % X, (x + 1 + 2 * core) % X
    runs = (
        ((each, x, 0), (each, near, 0)),
        ((part, far, core * part), (each, away, 0), (part, far, (1 - core) * part)),
    )
    own = tag_ref.shape[1] // each
    shards = tag_ref.shape[0] // X

    @pl.when(step == 0)
    def _():
        for total_ref in total_refs:
            total_ref[...] = jnp.zeros_like(total_ref)

    turn = 0
    for w in range(terms):
        row = step * (terms // own) + w // own
        for half_ref, some in zip((half_a, half_b), runs, strict=True):
            number = half_ref.shape[0]
            lhs = half_ref[:, w].reshape(number * rows, width)
            full = jnp.dot(lhs, right_ref[w], preferred_element_type=F32).astype(BF16)
            full = full.astype(F32).reshape(number, rows, width)
            s = 0
            for length, shard, first in some:
                for k in range(length):
                    t = tag_ref[shard * shards + row, w % own * each + first + k] - xb * count
                    t = jnp.where((t >= 0) & (t < count), t, count)
                    total_ref = total_refs[turn % len(total_refs)]
                    total_ref[t] += full[s]
                    s += 1
                    turn += 1

    @pl.when(step == pl.num_programs(0) - 1)
    def _():
        total = total_refs[0][:count]
        for total_ref in total_refs[1:]:
            total = total + total_ref[:count]
        out_ref[...] = total.astype(BF16)


def sums(place, tags, half_a, half_b, rights, count, steps):
    _, terms, rows, width = half_a.shape
    each = terms // steps
    pairs = terms * (half_a.shape[0] + half_b.shape[0])
    return pl.pallas_call(
        sums_kernel,
        grid_spec=pltpu.PrefetchScalarGridSpec(
            num_scalar_prefetch=2,
            grid=(steps,),
            in_specs=[
                pl.BlockSpec((h.shape[0], each, rows, width), lambda i, *_: (0, i, 0, 0))
                for h in (half_a, half_b)
            ]
            + [pl.BlockSpec((each, width, width), lambda i, *_: (i, 0, 0))],
            out_specs=pl.BlockSpec((count, rows, width), lambda i, *_: (0, 0, 0)),
            scratch_shapes=[pltpu.VMEM((count + 1, rows, width), F32)] * 2,
        ),
        out_shape=jax.ShapeDtypeStruct((count, rows, width), BF16),
        compiler_params=pltpu.CompilerParams(vmem_limit_bytes=56 << 20),
        cost_estimate=pl.CostEstimate(
            flops=2 * pairs * rows * width * width,
            bytes_accessed=2 * width * (pairs * rows + terms * width),
            transcendentals=0,
        ),
        name="sums",
    )(place, tags, half_a, half_b, rights)


def moved(block, axis, size, by):
    return lax.ppermute(block, axis, [(i, (i + by) % size) for i in range(size)])


def both_ways(block, by):
    pairs = []
    for i in range(X):
        pairs.append((i * C, (i + by) % X * C))
        pairs.append((i * C + 1, (i - by) % X * C + 1))
    return lax.ppermute(block, (*AXIS_X, "c"), pairs)


def added(parts):
    total = parts[0].astype(F32)
    for i in range(1, parts.shape[0]):
        total = total + parts[i].astype(F32)
    return total


def on_device(psi_blocks, left_env, right_env, dest_index, dest_slot):
    sectors, width = psi_blocks.shape[:2]
    terms = left_env.shape[0] // XA
    shards = Y * C
    rows = width // shards
    part = sectors // C
    xb, xa, core = lax.axis_index("xb"), lax.axis_index("xa"), lax.axis_index("c")
    right = lax.dynamic_slice_in_dim(right_env, xa * terms, terms, 0)
    rights = lax.all_gather(right, MPO, axis=0, tiled=True)
    target = (dest_index[0, 0, :, 0] * sectors + dest_slot[0, 0]).reshape(1, XA, 1, -1)
    target = jnp.broadcast_to(target, (XB, XA, shards, terms * sectors))
    tags = lax.all_to_all(
        target.reshape(X * shards, -1), (*AXIS_X, *MPO), split_axis=0, concat_axis=0, tiled=True
    )
    psi_next = both_ways(psi_blocks, 1)
    left = lax.dynamic_slice_in_dim(left_env, xa * terms, terms, 0)
    left = left.reshape(terms, shards, rows, width).transpose(1, 0, 2, 3)
    left = left.reshape(shards, terms * rows, width)
    tags, psi_next, left = lax.optimization_barrier((tags, psi_next, left))
    lefts = lax.all_to_all(left, MPO, split_axis=0, concat_axis=0, tiled=True)
    psi_far = both_ways(lax.dynamic_slice_in_dim(psi_next, core * part, part, 0), 1)
    place = jnp.stack([xb * XA + xa, core]).astype(jnp.int32)
    lefts = lefts.reshape(shards * terms * rows, width)
    half_a = halves(lefts, [psi_blocks, psi_next], shards * terms)
    rest = [psi_far, moved(psi_next, "c", C, 1), moved(psi_far, "c", C, 1)]
    half_b = halves(lefts, rest, shards * terms)
    partial = sums(place, tags, half_a, half_b, rights, XA * Z * sectors, STEPS)
    partial = partial.reshape(XA * Z, sectors, rows, width)
    partial = lax.all_to_all(partial, ("xa", "z"), split_axis=0, concat_axis=0, tiled=True)
    return added(partial)


def solution(mesh):
    chips = Mesh(mesh.devices.reshape(XB, XA, Z, Y, C), (*SEC, *MPO))
    in_specs = (
        P(SEC, None, None),
        P(MPO, None, None),
        P(MPO, None, None),
        P(MPO, SEC, None, None),
        P(MPO, SEC, None),
    )
    out_specs = P(SEC, MPO, None)
    return jax.shard_map(
        on_device, mesh=chips, in_specs=in_specs, out_specs=out_specs, check_vma=False
    )
```

```python
import jax
import jax.numpy as jnp
from jax import lax
from jax.experimental import pallas as pl
from jax.experimental.pallas import tpu as pltpu
from jax.sharding import Mesh
from jax.sharding import PartitionSpec as P

XB, XA, Z, Y, C = 2, 2, 8, 8, 2
X = XB * XA
AXIS_X, SEC, MPO = ("xb", "xa"), ("xb", "xa", "z"), ("y", "c")
BF16, F32 = jnp.bfloat16, jnp.float32
STEPS = 2


def half_kernel(left_ref, *refs):
    psi_refs, (half_ref, held_ref, sems) = refs[:-3], refs[-3:]
    _, terms, rows, width = held_ref.shape
    lefts = left_ref[...]
    copies = []
    for psi_ref in psi_refs:
        for k in range(psi_ref.shape[0]):
            at = len(copies)
            out = jnp.dot(lefts, psi_ref[k], preferred_element_type=F32).astype(BF16)
            held_ref[at] = out.reshape(terms, rows, width)
            copies.append(pltpu.make_async_copy(held_ref.at[at], half_ref.at[at], sems.at[at]))
            copies[-1].start()
    for copy in copies:
        copy.wait()


def halves(lefts, pieces, terms):
    count = sum(p.shape[0] for p in pieces)
    width = lefts.shape[1]
    rows = lefts.shape[0] // terms
    return pl.pallas_call(
        half_kernel,
        in_specs=[pl.BlockSpec(memory_space=pltpu.VMEM)] * (1 + len(pieces)),
        out_specs=pl.BlockSpec(memory_space=pltpu.HBM),
        out_shape=pltpu.HBM((count, terms, rows, width), BF16),
        scratch_shapes=[
            pltpu.VMEM((count, terms, rows, width), BF16),
            pltpu.SemaphoreType.DMA((count,)),
        ],
        compiler_params=pltpu.CompilerParams(vmem_limit_bytes=16 << 20),
        cost_estimate=pl.CostEstimate(
            flops=2 * terms * rows * width * width * count,
            bytes_accessed=2 * count * width * (width + terms * rows),
            transcendentals=0,
        ),
        name="halves",
    )(lefts, *pieces)


def sums_kernel(place_ref, tag_ref, half_a, half_b, right_ref, out_ref, *total_refs):
    step = pl.program_id(0)
    sectors_a, terms, rows, width = half_a.shape
    sectors_b = half_b.shape[0]
    x, core = place_ref[0], place_ref[1]
    xb = x // XA
    count = out_ref.shape[0]
    each = (sectors_a + sectors_b) // X
    part = each // C
    near, far, away = (x + X - 1 + 2 * core) % X, (x + 2) % X, (x + 1 + 2 * core) % X
    runs = (
        ((each, x, 0), (each, near, 0)),
        ((part, far, core * part), (each, away, 0), (part, far, (1 - core) * part)),
    )
    own = tag_ref.shape[1] // each
    shards = tag_ref.shape[0] // X

    @pl.when(step == 0)
    def _():
        for total_ref in total_refs:
            total_ref[...] = jnp.zeros_like(total_ref)

    turn = 0
    for w in range(terms):
        row = step * (terms // own) + w // own
        for half_ref, some in zip((half_a, half_b), runs, strict=True):
            number = half_ref.shape[0]
            lhs = half_ref[:, w].reshape(number * rows, width)
            full = jnp.dot(lhs, right_ref[w], preferred_element_type=F32).astype(BF16)
            full = full.astype(F32).reshape(number, rows, width)
            s = 0
            for length, shard, first in some:
                for k in range(length):
                    t = tag_ref[shard * shards + row, w % own * each + first + k] - xb * count
                    t = jnp.where((t >= 0) & (t < count), t, count)
                    total_ref = total_refs[turn % len(total_refs)]
                    total_ref[t] += full[s]
                    s += 1
                    turn += 1

    @pl.when(step == pl.num_programs(0) - 1)
    def _():
        total = total_refs[0][:count]
        for total_ref in total_refs[1:]:
            total = total + total_ref[:count]
        out_ref[...] = total.astype(BF16)


def sums(place, tags, half_a, half_b, rights, count, steps):
    _, terms, rows, width = half_a.shape
    each = terms // steps
    pairs = terms * (half_a.shape[0] + half_b.shape[0])
    return pl.pallas_call(
        sums_kernel,
        grid_spec=pltpu.PrefetchScalarGridSpec(
            num_scalar_prefetch=2,
            grid=(steps,),
            in_specs=[
                pl.BlockSpec((h.shape[0], each, rows, width), lambda i, *_: (0, i, 0, 0))
                for h in (half_a, half_b)
            ]
            + [pl.BlockSpec((each, width, width), lambda i, *_: (i, 0, 0))],
            out_specs=pl.BlockSpec((count, rows, width), lambda i, *_: (0, 0, 0)),
            scratch_shapes=[pltpu.VMEM((count + 1, rows, width), F32)] * 2,
        ),
        out_shape=jax.ShapeDtypeStruct((count, rows, width), BF16),
        compiler_params=pltpu.CompilerParams(vmem_limit_bytes=56 << 20),
        cost_estimate=pl.CostEstimate(
            flops=2 * pairs * rows * width * width,
            bytes_accessed=2 * width * (pairs * rows + terms * width),
            transcendentals=0,
        ),
        name="sums",
    )(place, tags, half_a, half_b, rights)


def moved(block, axis, size, by):
    return lax.ppermute(block, axis, [(i, (i + by) % size) for i in range(size)])


def both_ways(block, by):
    pairs = []
    for i in range(X):
        pairs.append((i * C, (i + by) % X * C))
        pairs.append((i * C + 1, (i - by) % X * C + 1))
    return lax.ppermute(block, (*AXIS_X, "c"), pairs)


def added(parts):
    total = parts[0].astype(F32)
    for i in range(1, parts.shape[0]):
        total = total + parts[i].astype(F32)
    return total


def on_device(psi_blocks, left_env, right_env, dest_index, dest_slot):
    sectors, width = psi_blocks.shape[:2]
    terms = left_env.shape[0] // XA
    shards = Y * C
    rows = width // shards
    part = sectors // C
    xb, xa, core = lax.axis_index("xb"), lax.axis_index("xa"), lax.axis_index("c")
    right = lax.dynamic_slice_in_dim(right_env, xa * terms, terms, 0)
    rights = lax.all_gather(right, MPO, axis=0, tiled=True)
    left = lax.dynamic_slice_in_dim(left_env, xa * terms, terms, 0)
    left = left.reshape(terms, shards, rows, width).transpose(1, 0, 2, 3)
    left = left.reshape(shards, terms * rows, width)
    lefts = lax.all_to_all(left, MPO, split_axis=0, concat_axis=0, tiled=True)
    psi_next = both_ways(psi_blocks, 1)
    target = dest_index[0, 0, :, 0] * sectors + dest_slot[0, 0]
    lefts, psi_next, target = lax.optimization_barrier((lefts, psi_next, target))
    psi_far = both_ways(lax.dynamic_slice_in_dim(psi_next, core * part, part, 0), 1)
    target = jnp.broadcast_to(
        target.reshape(1, XA, 1, terms * sectors), (XB, XA, shards, terms * sectors)
    )
    tags = lax.all_to_all(
        target.reshape(X * shards, -1), (*AXIS_X, *MPO), split_axis=0, concat_axis=0, tiled=True
    )
    place = jnp.stack([xb * XA + xa, core]).astype(jnp.int32)
    lefts = lefts.reshape(shards * terms * rows, width)
    half_a = halves(lefts, [psi_blocks, psi_next], shards * terms)
    rest = [psi_far, moved(psi_next, "c", C, 1), moved(psi_far, "c", C, 1)]
    half_b = halves(lefts, rest, shards * terms)
    partial = sums(place, tags, half_a, half_b, rights, XA * Z * sectors, STEPS)
    partial = partial.reshape(XA * Z, sectors, rows, width)
    partial = lax.all_to_all(partial, ("xa", "z"), split_axis=0, concat_axis=0, tiled=True)
    return added(partial)


def solution(mesh):
    chips = Mesh(mesh.devices.reshape(XB, XA, Z, Y, C), (*SEC, *MPO))
    in_specs = (
        P(SEC, None, None),
        P(MPO, None, None),
        P(MPO, None, None),
        P(MPO, SEC, None, None),
        P(MPO, SEC, None),
    )
    out_specs = P(SEC, MPO, None)
    return jax.shard_map(
        on_device, mesh=chips, in_specs=in_specs, out_specs=out_specs, check_vma=False
    )
```
